1024 devices in a mesh: rep: 8 (over x), ctx: 32 (over z, y_hi), head: 2 (over y_lo), pool: 2 (over core).
Axes of the slice: x: 8, y: 8 (y_hi: 4, y_lo: 2; y = y_hi * 2 + y_lo), z: 8, core: 2. Of those that a mesh axis runs over, the one named last changes fastest.
Arguments:
- prefix_kv: bfloat16 [32768, 4, 2, 128], P(('rep', 'ctx', 'head', 'pool')), may hold values from -24 to 24
- queries: bfloat16 [2, 2048, 32, 128], P(None, ('rep', 'ctx', 'pool'), 'head'), may hold values from -12 to 12
- suffix_cache: bfloat16 [2048, 512, 4, 2, 128], P(('rep', 'ctx', 'pool'), None, 'head'), may hold values from -8 to 8
- suffix_lengths: int32 [2048], P(('rep', 'ctx', 'pool')), may hold values from 1 to 510, as said below
Outputs:
- attention: bfloat16 [2, 2048, 32, 128], P(None, ('rep', 'ctx', 'pool'), 'head')
The draws below stay inside these ranges and needn't reach their ends.
Inputs may be any that keep to these rules, and one draw needn't show every extreme that they name: `suffix_lengths`: some session holds exactly 510 cached tokens, so that the last step of that session reads every slot.
All inputs are finite; a program needn't handle non-finite values.
Results may differ from the reference program's by a relative error of at most 0.0049.
Values may be sent and summed in bfloat16 or wider, within the bound.
A program may use at most 32 MiB of HBM per device.

```python
import math
import jax
import jax.numpy as jnp
from jax import lax

HD = 128
KVH = 4
GROUP = 8
STEPS = 2
SUF = 512
PIECE = 32
QH = 32
PREFIX = 32768
SESSIONS = 2048
N_REP = 8
N_CTX = 32
N_HEAD = 2
N_POOL = 2


def anchor_vectors(key):
    anchor_key = jax.random.fold_in(key, 11)
    signs = jax.random.bernoulli(anchor_key, 0.5, (KVH, HD))
    return jnp.where(signs, 2.0, -2.0).astype(jnp.float32)


def draw_prefix_kv(key, part):
    base_key = jax.random.fold_in(key, 21)
    key_one = jax.random.fold_in(base_key, 1)
    key_two = jax.random.fold_in(base_key, 2)
    row_shape = (PREFIX, KVH, HD)
    key_rows = jax.random.normal(key_one, row_shape, jnp.float32)
    value_rows = 4.0 * jax.random.normal(key_two, row_shape, jnp.float32)
    key_rows = jnp.clip(key_rows, -8.0, 8.0)
    value_rows = jnp.clip(value_rows, -24.0, 24.0)
    anchor = anchor_vectors(key)
    key_rows = key_rows.at[PREFIX - 1].set(anchor).at[PREFIX - 2].set(anchor * 1.01)
    return jnp.stack([key_rows, value_rows], axis=2).astype(jnp.bfloat16)


def draw_queries(key, part):
    base_key = jax.random.fold_in(key, 5)
    full_shape = (STEPS, SESSIONS, QH, HD)
    values = jnp.clip(2.7 * jax.random.normal(base_key, full_shape, jnp.float32), -12.0, 12.0)
    return values.astype(jnp.bfloat16)


def draw_suffix_cache(key, part):
    base_key = jax.random.fold_in(key, 7)
    full_shape = (SESSIONS, SUF, KVH, 2, HD)
    values = jnp.clip(1.6 * jax.random.normal(base_key, full_shape, jnp.float32), -8.0, 8.0)
    anchor = anchor_vectors(key)
    planted_count = min(8, SESSIONS)
    first = jnp.broadcast_to(anchor[None], (planted_count, KVH, HD))
    values = values.at[:planted_count, 0, :, 0, :].set(first)
    values = values.at[:planted_count, 1, :, 0, :].set(first * 1.01)
    return values.astype(jnp.bfloat16)


def draw_suffix_lengths(key, part):
    base_key = jax.random.fold_in(key, 9)
    key_one = jax.random.fold_in(base_key, 1)
    key_two = jax.random.fold_in(base_key, 2)
    lengths = jax.random.randint(key_one, (SESSIONS,), 1, SUF - STEPS + 1, dtype=jnp.int32)
    chosen = jax.random.randint(key_two, (), 0, SESSIONS, dtype=jnp.int32)
    return lengths.at[chosen].set(SUF - STEPS)


def setup_inputs(seed: int = 0) -> dict:
    seeds = jax.random.split(jax.random.key(seed), 5)
    prefix_kv = draw_prefix_kv(jax.random.fold_in(seeds[4], 71), 0)
    queries = draw_queries(jax.random.fold_in(seeds[4], 71), 0)
    suffix_cache = draw_suffix_cache(jax.random.fold_in(seeds[4], 71), 0)
    suffix_lengths = draw_suffix_lengths(jax.random.fold_in(seeds[4], 71), 0)
    return {"prefix_kv": prefix_kv, "queries": queries, "suffix_cache": suffix_cache, "suffix_lengths": suffix_lengths}


def shard_partial(query_block, context):
    score_scale = 1.0 / math.sqrt(HD)
    key_rows = context[:, :, 0, :].astype(jnp.float32)
    value_rows = context[:, :, 1, :].astype(jnp.float32)
    scores = jnp.einsum('tbkgd,lkd->tbkgl', query_block.astype(jnp.float32), key_rows) * score_scale
    top_score = lax.optimization_barrier(jnp.max(scores, axis=-1))
    weights = jnp.exp(scores - top_score[..., None])
    weight_sum = lax.optimization_barrier(jnp.sum(weights, axis=-1))
    rounded = lax.optimization_barrier(weights.astype(jnp.bfloat16)).astype(jnp.float32)
    accum = jnp.einsum('tbkgl,lkd->tbkgd', rounded, value_rows)
    partial_value = (accum / weight_sum[..., None]).astype(jnp.bfloat16)
    return (partial_value, top_score + jnp.log(weight_sum))

def reference(prefix_kv, queries, suffix_cache, suffix_lengths):
    shards = prefix_kv.reshape(N_REP, N_CTX, N_HEAD, N_POOL, PIECE, KVH, 2, HD)
    shards = jnp.moveaxis(shards, 1, 0).reshape(N_CTX, N_REP * N_HEAD * N_POOL * PIECE, KVH, 2, HD)
    split_queries = queries.reshape(STEPS, SESSIONS, KVH, GROUP, HD)
    block_size = min(SESSIONS, 64)
    while SESSIONS % block_size:
        block_size -= 1
    block_count = SESSIONS // block_size
    blocks = jnp.moveaxis(split_queries.reshape(STEPS, block_count, block_size, KVH, GROUP, HD), 1, 0)

    def per_shard(carry, context):
        run_top, run_sum, run_den = carry
        partials, log_totals = lax.map(lambda query_block: shard_partial(query_block, context), blocks)
        partials = jnp.moveaxis(partials, 0, 1).reshape(STEPS, SESSIONS, KVH, GROUP, HD).astype(jnp.float32)
        log_totals = jnp.moveaxis(log_totals, 0, 1).reshape(STEPS, SESSIONS, KVH, GROUP)
        new_top = jnp.maximum(run_top, log_totals)
        keep_factor = jnp.exp(run_top - new_top)
        take_factor = jnp.exp(log_totals - new_top)
        new_sum = run_sum * keep_factor[..., None] + take_factor[..., None] * partials
        new_den = run_den * keep_factor + take_factor
        return ((new_top, new_sum, new_den), None)
    initial = (jnp.full((STEPS, SESSIONS, KVH, GROUP), -jnp.inf, jnp.float32), jnp.zeros((STEPS, SESSIONS, KVH, GROUP, HD), jnp.float32), jnp.zeros((STEPS, SESSIONS, KVH, GROUP), jnp.float32))
    (run_top, run_sum, run_den), unused = lax.scan(per_shard, initial, shards)
    score_scale = 1.0 / math.sqrt(HD)
    suffix_keys = suffix_cache[:, :, :, 0, :].astype(jnp.float32)
    suffix_values = suffix_cache[:, :, :, 1, :].astype(jnp.float32)
    suffix_scores = jnp.einsum('tskgd,sjkd->tskgj', split_queries.astype(jnp.float32), suffix_keys) * score_scale
    positions = jnp.arange(SUF, dtype=jnp.int32)
    last_pos = suffix_lengths[None, :] + jnp.arange(STEPS, dtype=jnp.int32)[:, None]
    visible = (positions[None, None, :] <= last_pos[:, :, None])[:, :, None, None, :]
    masked = jnp.where(visible, suffix_scores, -jnp.inf)
    suffix_top = lax.optimization_barrier(jnp.max(masked, axis=-1))
    suffix_weights = jnp.exp(masked - suffix_top[..., None])
    suffix_sum = lax.optimization_barrier(jnp.sum(suffix_weights, axis=-1))
    suffix_rounded = lax.optimization_barrier(suffix_weights.astype(jnp.bfloat16)).astype(jnp.float32)
    suffix_accum = jnp.einsum('tskgj,sjkd->tskgd', suffix_rounded, suffix_values)
    top_all = jnp.maximum(run_top, suffix_top)
    prefix_factor = jnp.exp(run_top - top_all)
    suffix_factor = jnp.exp(suffix_top - top_all)
    numerator = run_sum * prefix_factor[..., None] + suffix_factor[..., None] * suffix_accum
    denominator = run_den * prefix_factor + suffix_factor * suffix_sum
    result = numerator / denominator[..., None]
    return result.reshape(STEPS, SESSIONS, QH, HD).astype(jnp.bfloat16)
```

```python
import functools
import math

import jax
import jax.numpy as jnp
from jax import lax
from jax.experimental import pallas as pl
from jax.experimental.pallas import tpu as pltpu
from jax.sharding import PartitionSpec as P

MESH = pl.DeviceIdType.MESH
F32 = jnp.float32
BF16 = jnp.bfloat16
HD = 128
RING = 8
SCALE = 1.0 / math.sqrt(HD)
LOG2E = 1.0 / math.log(2.0)
ORDER = (0, 1, 7, 2, 6, 3, 5, 4)


def wrap(v):
    return lax.rem(v + 2 * RING, RING)


def kernel(
    pre_ref, q_ref, len_ref, suf_hbm, out_ref,
    kvbuf, kvf, kvsrc, qsrc, qbuf, sufbuf, top, tot, acc, osrc, lsrc, obuf, lbuf,
    sacc, smax, ssum, ob,
    suf_sem, send_sem, y_sem, q_sem, xr_sem, xl_sem, o_sem, l_sem,
):
    x = lax.axis_index("rep")
    c = lax.axis_index("ctx")
    hd = lax.axis_index("head")
    core = lax.axis_index("pool")
    z = lax.div(c, 4)
    y = lax.rem(c, 4) * 2 + hd

    def device(xx, yy, zz, cc):
        return (xx, zz * 4 + lax.div(yy, 2), lax.rem(yy, 2), cc)

    ypeers = [(i, d, cc) for i, d in enumerate(ORDER) for cc in (0, 1) if (d, cc) != (0, 0)]
    zpeers = [(d, cc) for d in ORDER for cc in (0, 1) if (d, cc) != (0, 0)]

    def other(cc):
        return lax.rem(core + cc, 2)

    barrier = pltpu.get_barrier_semaphore()
    greet = [device(x, wrap(y + d), z, other(cc)) for _, d, cc in ypeers]
    greet += [device(x, y, wrap(z + d), other(cc)) for d, cc in zpeers if d]
    greet += [device(wrap(x + 1), y, z, core), device(wrap(x - 1), y, z, core)]
    for dev in greet:
        pl.semaphore_signal(barrier, inc=1, device_id=dev, device_id_type=MESH)

    suffix_copy = pltpu.make_async_copy(suf_hbm, sufbuf, suf_sem)
    suffix_copy.start()

    kvf[...] = pre_ref[...].astype(F32)
    for r in range(8):
        kvsrc[r // 2, r % 2] = kvf[pl.ds(r, 32, stride=8), :].astype(BF16)
    my_head = 2 * hd + core
    kvbuf[x, 0] = kvsrc[my_head]
    q8 = q_ref[...].reshape(8, 16, HD).astype(F32)
    for k in range(2):
        qsrc[k] = q8[:, 8 * k : 8 * k + 8, :].reshape(64, HD).astype(BF16)
    qbuf[0] = qsrc[core]
    top[...] = jnp.full_like(top, -jnp.inf)
    tot[...] = jnp.zeros_like(tot)
    acc[...] = jnp.zeros_like(acc)

    pl.semaphore_wait(barrier, len(greet))

    sends = []

    def remote(src, dst, recv, dev):
        copy = pltpu.make_async_remote_copy(
            src_ref=src, dst_ref=dst, send_sem=send_sem.at[len(sends)], recv_sem=recv,
            device_id=dev, device_id_type=MESH,
        )
        copy.start()
        sends.append(copy)

    slot_of = {d: i for i, d in enumerate(ORDER)}
    for i, d, cc in ypeers:
        yy, pc = wrap(y + d), other(cc)
        slot = slot_of[(-d) % RING] * 2 + cc
        remote(
            kvsrc.at[2 * lax.rem(yy, 2) + pc], kvbuf.at[x, slot],
            y_sem.at[slot // 4], device(x, yy, z, pc),
        )
    for d, cc in zpeers:
        pc = other(cc)
        slot = ((-d) % RING) * 2 + cc
        remote(qsrc.at[pc], qbuf.at[slot], q_sem, device(x, y, wrap(z + d), pc))

    suffix_copy.wait()
    row = lax.broadcasted_iota(jnp.int32, (32, 2048), 0)
    col = lax.broadcasted_iota(jnp.int32, (32, 2048), 1)
    base_ok = jnp.logical_and((col & 1) == 0, ((col >> 1) & 1) == ((row >> 3) & 1))
    reach = (col >> 2) - (row >> 4)
    for n in range(4):
        kv = sufbuf[n]
        qn = q_ref[:, n].reshape(32, HD)
        s = lax.dot_general(qn, kv, (((1,), (1,)), ((), ())), preferred_element_type=F32)
        ok = jnp.logical_and(base_ok, reach <= len_ref[n])
        s = jnp.where(ok, s, -jnp.inf)
        mx = jnp.max(s, axis=1, keepdims=True)
        p = jnp.exp2((s - mx) * (SCALE * LOG2E))
        sm = jnp.sum(p, axis=1, keepdims=True)
        pb = pltpu.roll(p, 1, 1).astype(BF16)
        a = jnp.dot(pb, kv, preferred_element_type=F32)
        mxb = jnp.broadcast_to(mx * SCALE, (32, HD))
        smb = jnp.broadcast_to(sm, (32, HD))
        for t in range(2):
            for k in range(2):
                lo = 16 * t + 8 * k
                sacc[k, 4 * t + n] = a[lo : lo + 8]
                smax[k, 4 * t + n] = mxb[lo : lo + 8]
                ssum[k, 4 * t + n] = smb[lo : lo + 8]

    right, left = device(wrap(x + 1), y, z, core), device(wrap(x - 1), y, z, core)

    def hop(i, slot, g, to_right):
        sem = xr_sem if to_right else xl_sem
        ref = kvbuf.at[slot, pl.ds(4 * g, 4)]
        return pltpu.make_async_remote_copy(
            src_ref=ref, dst_ref=ref, send_sem=sem.at[0, i], recv_sem=sem.at[1, i],
            device_id=right if to_right else left, device_id_type=MESH,
        )

    def unit(sa, ga, sb, gb):
        def part(slot, g, which):
            return kvbuf[slot, pl.ds(4 * g, 4), which].reshape(128, HD)

        k = jnp.concatenate([part(sa, ga, 0), part(sb, gb, 0)], axis=0)
        v = jnp.concatenate([part(sa, ga, 1), part(sb, gb, 1)], axis=0)

        def rows(i, carry):
            r = pl.ds(pl.multiple_of(i * 256, 256), 256)
            q = qbuf[pl.ds(4 * i, 4)].reshape(256, HD)
            s = lax.dot_general(q, k, (((1,), (1,)), ((), ())), preferred_element_type=F32)
            old = top[r, :]
            new = jnp.maximum(old, jnp.max(s, axis=1, keepdims=True))
            p = jnp.exp2((s - jnp.concatenate([new, new], axis=1)) * (SCALE * LOG2E))
            keep = jnp.exp2((old - new) * (SCALE * LOG2E))
            top[r, :] = new
            tot[r, :] = tot[r, :] * keep + (p[:, :128] + p[:, 128:])
            acc[r, :] = acc[r, :] * keep + jnp.dot(p.astype(BF16), v, preferred_element_type=F32)
            return carry

        lax.fori_loop(0, 4, rows, 0)

    for g in range(4):
        lo = 1 if g == 0 else 4 * g
        piece = kvbuf.at[x, pl.ds(lo, 4 * g + 4 - lo)]
        pltpu.make_async_copy(piece, piece, y_sem.at[g]).wait()
        hop(g, x, g, True).start()
        hop(g, x, g, False).start()
    pltpu.make_async_copy(qbuf.at[pl.ds(1, 15)], qbuf.at[pl.ds(1, 15)], q_sem).wait()
    unit(x, 0, x, 1)
    unit(x, 2, x, 3)

    def middle(i, carry):
        h = lax.div(i, 4) + 1
        g = lax.rem(i, 4)
        sl, sr = wrap(x - h), wrap(x + h)
        hop(i, sl, g, True).wait_recv()

        @pl.when(jnp.logical_or(h < 3, g < 2))
        def _():
            hop(i + 4, sl, g, True).start()

        hop(i, sr, g, False).wait_recv()

        @pl.when(h < 3)
        def _():
            hop(i + 4, sr, g, False).start()

        @pl.when(jnp.logical_and(h == 3, g >= 2))
        def _():
            hop(i + 2, sr, g, False).start()

        unit(sl, g, sr, g)
        return carry

    lax.fori_loop(0, 12, middle, 0)
    far = wrap(x + 4)
    for g in range(2):
        hop(12 + g, far, g, True).wait_recv()
        hop(12 + g, far, g + 2, False).wait_recv()
        unit(far, g, far, g + 2)

    eye = lax.broadcasted_iota(jnp.int32, (64, HD), 0) == lax.broadcasted_iota(
        jnp.int32, (64, HD), 1
    )

    def finish(s):
        r = pl.ds(64 * s, 64)
        whole = jnp.sum(tot[r, :], axis=1, keepdims=True)
        osrc[s] = (acc[r, :] / whole).astype(BF16)
        lse = top[r, :] * SCALE + jnp.log(whole)
        lsrc[s] = jnp.sum(jnp.where(eye, lse, 0.0), axis=0, keepdims=True)

    def give(d, cc):
        pc, s = other(cc), 2 * d + cc
        dev = device(x, y, wrap(z + d), pc)
        slot = ((-d) % RING) * 2 + cc
        remote(lsrc.at[s], lbuf.at[slot], l_sem, dev)
        remote(osrc.at[s], obuf.at[slot], o_sem, dev)

    order = list(reversed(zpeers))
    finish(2 * order[0][0] + order[0][1])
    for here, after in zip(order, order[1:] + [(0, 0)]):
        finish(2 * after[0] + after[1])
        give(*here)
    obuf[0] = osrc[0]
    lbuf[0] = lsrc[0]

    pltpu.make_async_copy(lbuf.at[pl.ds(1, 15)], lbuf.at[pl.ds(1, 15)], l_sem).wait()
    pltpu.make_async_copy(obuf.at[pl.ds(1, 15)], obuf.at[pl.ds(1, 15)], o_sem).wait()
    for kk in range(2):
        k = other(kk)
        sx = smax[k].reshape(64, HD)
        lses = []
        for d in range(RING):
            spread = jnp.where(eye, lbuf[2 * d + kk], 0.0)
            lses.append(jnp.sum(spread, axis=1, keepdims=True))
        best = sx
        for v in lses:
            best = jnp.maximum(best, v)
        w = jnp.exp2((sx - best) * LOG2E)
        num = w * sacc[k].reshape(64, HD)
        den = w * ssum[k].reshape(64, HD)
        for d in range(RING):
            w = jnp.exp2((lses[d] - best) * LOG2E)
            num = num + w * obuf[2 * d + kk].astype(F32)
            den = den + w
        ob[k] = (num / den).reshape(8, 8, HD)
    both = jnp.stack([ob[0], ob[1]], axis=1).reshape(8, 16, HD)
    out_ref[...] = both.astype(BF16).reshape(2, 4, 16, HD)

    for copy in sends:
        copy.wait_send()

    def drain(i, carry):
        hop(i, x, 0, True).wait_send()
        hop(i, x, 0, False).wait_send()
        return carry

    lax.fori_loop(0, 14, drain, 0)


def local(prefix_kv, queries, suffix_cache, suffix_lengths):
    vmem = pl.BlockSpec(memory_space=pltpu.VMEM)
    dma = pltpu.SemaphoreType.DMA
    return pl.pallas_call(
        kernel,
        out_shape=jax.ShapeDtypeStruct(queries.shape, BF16),
        in_specs=[
            vmem, vmem, pl.BlockSpec(memory_space=pltpu.SMEM), pl.BlockSpec(memory_space=pl.ANY),
        ],
        out_specs=vmem,
        scratch_shapes=[
            pltpu.VMEM((8, 16, 2, 32, HD), BF16),
            pltpu.VMEM((256, HD), F32),
            pltpu.VMEM((4, 2, 32, HD), BF16),
            pltpu.VMEM((2, 64, HD), BF16),
            pltpu.VMEM((16, 64, HD), BF16),
            pltpu.VMEM((4, 2048, HD), BF16),
            pltpu.VMEM((1024, HD), F32),
            pltpu.VMEM((1024, HD), F32),
            pltpu.VMEM((1024, HD), F32),
            pltpu.VMEM((16, 64, HD), BF16),
            pltpu.VMEM((16, 1, HD), F32),
            pltpu.VMEM((16, 64, HD), BF16),
            pltpu.VMEM((16, 1, HD), F32),
            pltpu.VMEM((2, 8, 8, HD), F32),
            pltpu.VMEM((2, 8, 8, HD), F32),
            pltpu.VMEM((2, 8, 8, HD), F32),
            pltpu.VMEM((2, 8, 8, HD), F32),
            dma, dma((60,)), dma((4,)), dma, dma((2, 14)), dma((2, 14)), dma, dma,
        ],
        compiler_params=pltpu.CompilerParams(
            collective_id=0, has_side_effects=True, vmem_limit_bytes=48 * 1024 * 1024
        ),
    )(
        prefix_kv.reshape(256, HD), queries, suffix_lengths,
        suffix_cache.reshape(4, 2048, HD),
    )


def solution(mesh):
    return jax.shard_map(
        local,
        mesh=mesh,
        in_specs=(
            P(("rep", "ctx", "head", "pool"), None, None, None),
            P(None, ("rep", "ctx", "pool"), "head", None),
            P(("rep", "ctx", "pool"), None, "head", None, None),
            P(("rep", "ctx", "pool")),
        ),
        out_specs=P(None, ("rep", "ctx", "pool"), "head", None),
        check_vma=False,
    )
```

```python
import functools
import math

import jax
import jax.numpy as jnp
from jax import lax
from jax.experimental import pallas as pl
from jax.experimental.pallas import tpu as pltpu
from jax.sharding import PartitionSpec as P

MESH = pl.DeviceIdType.MESH
F32 = jnp.float32
BF16 = jnp.bfloat16
HD = 128
RING = 8
SCALE = 1.0 / math.sqrt(HD)
LOG2E = 1.0 / math.log(2.0)
ORDER = (0, 1, 7, 2, 6, 3, 5, 4)


def wrap(v):
    return lax.rem(v + 2 * RING, RING)


def kernel(
    pre_hbm, q_hbm, len_hbm, suf_hbm, out_ref,
    pre_ref, q_ref, len_ref, kvbuf, kvf, kvsrc, qsrc, qbuf, sufbuf, top, tot, acc, osrc, lsrc, obuf, lbuf,
    sacc, smax, ssum, ob,
    in_sem, send_sem, y_sem, q_sem, xr_sem, xl_sem, o_sem, l_sem,
):
    x = lax.axis_index("rep")
    c = lax.axis_index("ctx")
    hd = lax.axis_index("head")
    core = lax.axis_index("pool")
    z = lax.div(c, 4)
    y = lax.rem(c, 4) * 2 + hd

    def device(xx, yy, zz, cc):
        return (xx, zz * 4 + lax.div(yy, 2), lax.rem(yy, 2), cc)

    ypeers = [(i, d, cc) for i, d in enumerate(ORDER) for cc in (0, 1) if (d, cc) != (0, 0)]
    zpeers = [(d, cc) for d in ORDER for cc in (0, 1) if (d, cc) != (0, 0)]

    def other(cc):
        return lax.rem(core + cc, 2)

    fetch = [
        pltpu.make_async_copy(src, dst, in_sem.at[i])
        for i, (src, dst) in enumerate(
            [(pre_hbm, pre_ref), (q_hbm, q_ref), (len_hbm, len_ref), (suf_hbm, sufbuf)]
        )
    ]
    for copy in fetch:
        copy.start()

    barrier = pltpu.get_barrier_semaphore()
    greet = [device(x, wrap(y + d), z, other(cc)) for _, d, cc in ypeers]
    greet += [device(x, y, wrap(z + d), other(cc)) for d, cc in zpeers if d]
    greet += [device(wrap(x + 1), y, z, core), device(wrap(x - 1), y, z, core)]
    for dev in greet:
        pl.semaphore_signal(barrier, inc=1, device_id=dev, device_id_type=MESH)

    fetch[0].wait()
    fetch[1].wait()
    kvf[...] = pre_ref[...].astype(F32)
    for r in range(8):
        kvsrc[r // 2, r % 2] = kvf[pl.ds(r, 32, stride=8), :].astype(BF16)
    my_head = 2 * hd + core
    kvbuf[x, 0] = kvsrc[my_head]
    q8 = q_ref[...].reshape(8, 16, HD).astype(F32)
    for k in range(2):
        qsrc[k] = q8[:, 8 * k : 8 * k + 8, :].reshape(64, HD).astype(BF16)
    qbuf[2 * z] = qsrc[core]

    pl.semaphore_wait(barrier, len(greet))

    sends = []

    def remote(src, dst, recv, dev):
        copy = pltpu.make_async_remote_copy(
            src_ref=src, dst_ref=dst, send_sem=send_sem.at[len(sends)], recv_sem=recv,
            device_id=dev, device_id_type=MESH,
        )
        copy.start()
        sends.append(copy)

    slot_of = {d: i for i, d in enumerate(ORDER)}
    for i, d, cc in ypeers:
        yy, pc = wrap(y + d), other(cc)
        slot = slot_of[(-d) % RING] * 2 + cc
        remote(
            kvsrc.at[2 * lax.rem(yy, 2) + pc], kvbuf.at[x, slot],
            y_sem.at[slot // 4], device(x, yy, z, pc),
        )
    for d, cc in zpeers:
        pc = other(cc)
        remote(qsrc.at[pc], qbuf.at[2 * z + cc], q_sem, device(x, y, wrap(z + d), pc))

    right, left = device(wrap(x + 1), y, z, core), device(wrap(x - 1), y, z, core)

    def hop(i, slot, g, to_right):
        sem = xr_sem if to_right else xl_sem
        ref = kvbuf.at[slot, pl.ds(4 * g, 4)]
        return pltpu.make_async_remote_copy(
            src_ref=ref, dst_ref=ref, send_sem=sem.at[0, i], recv_sem=sem.at[1, i],
            device_id=right if to_right else left, device_id_type=MESH,
        )

    row = lax.broadcasted_iota(jnp.int32, (32, 2048), 0)
    col = lax.broadcasted_iota(jnp.int32, (32, 2048), 1)
    base_ok = jnp.logical_and((col & 1) == 0, ((col >> 1) & 1) == ((row >> 3) & 1))
    reach = (col >> 2) - (row >> 4)

    def suffix(n):
        kv = sufbuf[n]
        qn = q_ref[:, n].reshape(32, HD)
        s = lax.dot_general(qn, kv, (((1,), (1,)), ((), ())), preferred_element_type=F32)
        ok = jnp.logical_and(base_ok, reach <= len_ref[n])
        s = jnp.where(ok, s, -jnp.inf)
        mx = jnp.max(s, axis=1, keepdims=True)
        p = jnp.exp2((s - mx) * (SCALE * LOG2E))
        sm = jnp.sum(p, axis=1, keepdims=True)
        pb = pltpu.roll(p, 1, 1).astype(BF16)
        a = jnp.dot(pb, kv, preferred_element_type=F32)
        mxb = jnp.broadcast_to(mx * SCALE, (32, HD))
        smb = jnp.broadcast_to(sm, (32, HD))
        for t in range(2):
            for k in range(2):
                lo = 16 * t + 8 * k
                sacc[k, 4 * t + n] = a[lo : lo + 8]
                smax[k, 4 * t + n] = mxb[lo : lo + 8]
                ssum[k, 4 * t + n] = smb[lo : lo + 8]

    def unit(sa, ga, sb, gb, first=False, after=None):
        def part(slot, g, which):
            return kvbuf[slot, pl.ds(4 * g, 4), which].reshape(128, HD)

        k = jnp.concatenate([part(sa, ga, 0), part(sb, gb, 0)], axis=0)
        v = jnp.concatenate([part(sa, ga, 1), part(sb, gb, 1)], axis=0).T
        def scores(j):
            q = qbuf[4 * j : 4 * j + 4].reshape(256, HD)
            return lax.dot_general(k, q, (((1,), (1,)), ((), ())), preferred_element_type=F32)

        def weigh(j, s):
            r = pl.ds(256 * j, 256)
            new = jnp.max(s, axis=0, keepdims=True)
            keep = None
            if not first:
                old = top[:, r]
                new = jnp.maximum(old, new)
                keep = jnp.exp2((old - new) * (SCALE * LOG2E))
            p = jnp.exp2((s - new) * (SCALE * LOG2E))
            part_sum = jnp.sum(p.reshape(32, 8, 256), axis=0)
            if not first:
                part_sum = tot[:, r] * keep + part_sum
            top[:, r] = new
            tot[:, r] = part_sum
            return p.astype(BF16), keep

        def gather(j, p, keep):
            r = pl.ds(256 * j, 256)
            o = jnp.dot(v, p, preferred_element_type=F32)
            acc[:, r] = o if first else acc[:, r] * keep + o
            if after:
                after(j)

        js = (0, 1, 2, 3)
        s = scores(js[0])
        late = None
        for i, j in enumerate(js):
            s_next = scores(js[i + 1]) if i < 3 else None
            if late:
                gather(*late)
            late = (j, *weigh(j, s))
            s = s_next
        gather(*late)

    for g in range(4):
        lo = 1 if g == 0 else 4 * g
        piece = kvbuf.at[x, pl.ds(lo, 4 * g + 4 - lo)]
        pltpu.make_async_copy(piece, piece, y_sem.at[g]).wait()
        hop(g, x, g, True).start()
        hop(g, x, g, False).start()
        if g == 0:
            fetch[2].wait()
            fetch[3].wait()
        if g < 2:
            suffix(2 * g)
            suffix(2 * g + 1)
    pltpu.make_async_copy(qbuf.at[pl.ds(1, 15)], qbuf.at[pl.ds(1, 15)], q_sem).wait()
    unit(x, 0, x, 1, first=True)
    unit(x, 2, x, 3)

    def middle(i, carry):
        h = lax.div(i, 4) + 1
        g = lax.rem(i, 4)
        sl, sr = wrap(x - h), wrap(x + h)
        hop(i, sl, g, True).wait_recv()

        @pl.when(jnp.logical_or(h < 3, g < 2))
        def _():
            hop(i + 4, sl, g, True).start()

        hop(i, sr, g, False).wait_recv()

        @pl.when(h < 3)
        def _():
            hop(i + 4, sr, g, False).start()

        @pl.when(jnp.logical_and(h == 3, g >= 2))
        def _():
            hop(i + 2, sr, g, False).start()

        unit(sl, g, sr, g)
        return carry

    lax.fori_loop(0, 12, middle, 0)
    def finish(plane):
        r = pl.ds(128 * plane, 128)
        whole = jnp.sum(tot[:, r], axis=0, keepdims=True)
        lsrc[plane] = top[:, r] * SCALE + jnp.log(whole)
        osrc[pl.ds(2 * plane, 2)] = (acc[:, r] / whole).T.astype(BF16).reshape(2, 64, HD)

    def give(plane):
        for cc in range(2):

            def send():
                for src, dst, sem in (
                    (lsrc.at[plane], lbuf.at[2 * z + cc], l_sem),
                    (osrc.at[2 * plane + cc], obuf.at[2 * z + cc], o_sem),
                ):
                    pltpu.make_async_remote_copy(
                        src_ref=src, dst_ref=dst, send_sem=sem.at[0], recv_sem=sem.at[1],
                        device_id=device(x, y, plane, other(cc)), device_id_type=MESH,
                    ).start()

            if cc:
                send()
            else:
                pl.when(z != plane)(send)

    ready = []

    def after(j):
        held = list(ready)
        ready.clear()
        for plane in (2 * j, 2 * j + 1):
            finish(plane)
            ready.append(plane)
        for plane in held:
            give(plane)

    far = wrap(x + 4)
    for g in range(2):
        hop(12 + g, far, g, True).wait_recv()
        hop(12 + g, far, g + 2, False).wait_recv()
        unit(far, g, far, g + 2, after=after if g else None)
    obuf[2 * z] = osrc[2 * z]
    lbuf[2 * z] = lsrc[z]
    for plane in ready:
        give(plane)

    def all_of(ref, sem):
        rest = ref.at[pl.ds(0, 15)]
        return pltpu.make_async_copy(rest, rest, sem)

    all_of(lbuf, l_sem.at[1]).wait()
    all_of(obuf, o_sem.at[1]).wait()
    for kk in range(2):
        k = other(kk)
        eye = lax.broadcasted_iota(jnp.int32, (64, HD), 0) + 64 * kk == lax.broadcasted_iota(
            jnp.int32, (64, HD), 1
        )
        sx = smax[k].reshape(64, HD)
        lses = []
        for d in range(RING):
            spread = jnp.where(eye, lbuf[2 * d + kk], 0.0)
            lses.append(jnp.sum(spread, axis=1, keepdims=True))
        best = sx
        for v in lses:
            best = jnp.maximum(best, v)
        w = jnp.exp2((sx - best) * LOG2E)
        num = w * sacc[k].reshape(64, HD)
        den = w * ssum[k].reshape(64, HD)
        for d in range(RING):
            w = jnp.exp2((lses[d] - best) * LOG2E)
            num = num + w * obuf[2 * d + kk].astype(F32)
            den = den + w
        ob[k] = (num / den).reshape(8, 8, HD)
    both = jnp.stack([ob[0], ob[1]], axis=1).reshape(8, 16, HD)
    out_ref[...] = both.astype(BF16).reshape(2, 4, 16, HD)

    for copy in sends:
        copy.wait_send()
    all_of(lbuf, l_sem.at[0]).wait()
    all_of(obuf, o_sem.at[0]).wait()

    def drain(i, carry):
        hop(i, x, 0, True).wait_send()
        hop(i, x, 0, False).wait_send()
        return carry

    lax.fori_loop(0, 14, drain, 0)


def local(prefix_kv, queries, suffix_cache, suffix_lengths):
    vmem = pl.BlockSpec(memory_space=pltpu.VMEM)
    hbm = pl.BlockSpec(memory_space=pltpu.HBM)
    dma = pltpu.SemaphoreType.DMA
    return pl.pallas_call(
        kernel,
        out_shape=jax.ShapeDtypeStruct(queries.shape, BF16),
        in_specs=[
            hbm, hbm, hbm, hbm,
        ],
        out_specs=vmem,
        scratch_shapes=[
            pltpu.VMEM((256, HD), BF16),
            pltpu.VMEM((2, 4, 16, HD), BF16),
            pltpu.SMEM((4,), jnp.int32),
            pltpu.VMEM((8, 16, 2, 32, HD), BF16),
            pltpu.VMEM((256, HD), F32),
            pltpu.VMEM((4, 2, 32, HD), BF16),
            pltpu.VMEM((2, 64, HD), BF16),
            pltpu.VMEM((16, 64, HD), BF16),
            pltpu.VMEM((4, 2048, HD), BF16),
            pltpu.VMEM((1, 1024), F32),
            pltpu.VMEM((8, 1024), F32),
            pltpu.VMEM((HD, 1024), F32),
            pltpu.VMEM((16, 64, HD), BF16),
            pltpu.VMEM((8, 1, HD), F32),
            pltpu.VMEM((16, 64, HD), BF16),
            pltpu.VMEM((16, 1, HD), F32),
            pltpu.VMEM((2, 8, 8, HD), F32),
            pltpu.VMEM((2, 8, 8, HD), F32),
            pltpu.VMEM((2, 8, 8, HD), F32),
            pltpu.VMEM((2, 8, 8, HD), F32),
            dma((4,)), dma((30,)), dma((4,)), dma, dma((2, 14)), dma((2, 14)), dma((2,)), dma((2,)),
        ],
        compiler_params=pltpu.CompilerParams(
            collective_id=0, has_side_effects=True, vmem_limit_bytes=66961408
        ),
    )(
        prefix_kv.reshape(256, HD), queries, suffix_lengths,
        suffix_cache.reshape(4, 2048, HD),
    )


def solution(mesh):
    return jax.shard_map(
        local,
        mesh=mesh,
        in_specs=(
            P(("rep", "ctx", "head", "pool"), None, None, None),
            P(None, ("rep", "ctx", "pool"), "head", None),
            P(("rep", "ctx", "pool"), None, "head", None, None),
            P(("rep", "ctx", "pool")),
        ),
        out_specs=P(None, ("rep", "ctx", "pool"), "head", None),
        check_vma=False,
    )
```

```python
import functools
import math

import jax
import jax.numpy as jnp
from jax import lax
from jax.experimental import pallas as pl
from jax.experimental.pallas import tpu as pltpu
from jax.sharding import PartitionSpec as P

MESH = pl.DeviceIdType.MESH
F32 = jnp.float32
BF16 = jnp.bfloat16
HD = 128
RING = 8
SCALE = 1.0 / math.sqrt(HD)
LOG2E = 1.0 / math.log(2.0)
ORDER = (0, 1, 7, 2, 6, 3, 5, 4)


def wrap(v):
    return lax.rem(v + 2 * RING, RING)


def kernel(
    pre_hbm, q_hbm, len_hbm, suf_hbm, out_ref,
    pre_ref, q_ref, len_ref, kvbuf, kvs, xbuf, kvf, kvsrc, qsrc, qbuf, sufbuf, top, tot, acc, osrc, lsrc, obuf, lbuf,
    sacc, smax, ssum, ob,
    in_sem, send_sem, ys_sem, f_sem, sd_sem, s_sem, y_sem, q_sem, xr_sem, xl_sem, o_sem, l_sem,
):
    x = lax.axis_index("rep")
    c = lax.axis_index("ctx")
    hd = lax.axis_index("head")
    core = lax.axis_index("pool")
    z = lax.div(c, 4)
    y = lax.rem(c, 4) * 2 + hd

    def device(xx, yy, zz, cc):
        return (xx, zz * 4 + lax.div(yy, 2), lax.rem(yy, 2), cc)

    ypeers = [(i, d, cc) for i, d in enumerate(ORDER) for cc in (0, 1) if (d, cc) != (0, 0)]
    zpeers = [(d, cc) for d in ORDER for cc in (0, 1) if (d, cc) != (0, 0)]

    def other(cc):
        return lax.rem(core + cc, 2)

    fetch = [
        pltpu.make_async_copy(src, dst, in_sem.at[i])
        for i, (src, dst) in enumerate(
            [(pre_hbm, pre_ref), (q_hbm, q_ref), (len_hbm, len_ref), (suf_hbm, sufbuf)]
        )
    ]
    for copy in fetch:
        copy.start()

    barrier = pltpu.get_barrier_semaphore()
    greet = [device(x, wrap(y + d), z, other(cc)) for _, d, cc in ypeers]
    greet += [device(x, y, wrap(z + d), other(cc)) for d, cc in zpeers if d]
    greet += [device(wrap(x + 1), y, z, core), device(wrap(x - 1), y, z, core)]
    for dev in greet:
        pl.semaphore_signal(barrier, inc=1, device_id=dev, device_id_type=MESH)

    fetch[0].wait()
    fetch[1].wait()
    kvf[...] = pre_ref[...].astype(F32)
    for r in range(8):
        kvsrc[r // 2, r % 2] = kvf[pl.ds(r, 32, stride=8), :].astype(BF16)
    my_head = 2 * hd + core
    q8 = q_ref[...].reshape(8, 16, HD).astype(F32)
    for k in range(2):
        qsrc[k] = q8[:, 8 * k : 8 * k + 8, :].reshape(64, HD).astype(BF16)
    qbuf[2 * z] = qsrc[core]

    pl.semaphore_wait(barrier, len(greet))

    sends = []

    def remote(src, dst, recv, dev):
        copy = pltpu.make_async_remote_copy(
            src_ref=src, dst_ref=dst, send_sem=send_sem.at[len(sends)], recv_sem=recv,
            device_id=dev, device_id_type=MESH,
        )
        copy.start()
        sends.append(copy)

    slot_of = {d: i for i, d in enumerate(ORDER)}
    right, left = device(wrap(x + 1), y, z, core), device(wrap(x - 1), y, z, core)

    for cr, (src_rows, dst_rows) in enumerate(((32, 0), (16, 32))):

        @pl.when(core == cr)
        def _():
            for d in ORDER:
                for pc in (cr, 1 - cr):
                    yy = wrap(y + d)
                    src = kvsrc.at[2 * lax.rem(yy, 2) + pc, :, pl.ds(0, src_rows)]
                    slot = slot_of[(-d) % RING]
                    dst = kvbuf.at[x, slot, :, pl.ds(dst_rows, src_rows)]
                    sem = y_sem.at[slot // 2]
                    if (d, pc) == (0, cr):
                        pltpu.make_async_copy(src, dst, sem).start()
                    else:
                        pltpu.make_async_remote_copy(
                            src_ref=src, dst_ref=dst, send_sem=ys_sem, recv_sem=sem,
                            device_id=device(x, yy, z, pc), device_id_type=MESH,
                        ).start()

    late_rows = pl.ds(16, 16)

    def first(i, block, to_right):
        way = 0 if to_right else 1
        ref = xbuf.at[pl.ds(4 * block, 4)]
        return pltpu.make_async_remote_copy(
            src_ref=kvsrc.at[:, :, late_rows] if i == 0 else ref, dst_ref=ref,
            send_sem=f_sem.at[way, 0, i], recv_sem=f_sem.at[way, 1, i],
            device_id=right if to_right else left, device_id_type=MESH,
        )

    def spread(block, own=False):
        for d in ORDER:
            yy = wrap(y + d)
            slot = slot_of[(-d) % RING]
            for pc in (1, 0):
                head = 2 * lax.rem(yy, 2) + pc
                src = kvsrc.at[head, :, late_rows] if own else xbuf.at[4 * block + head]
                dst, sem = kvs.at[block, slot], s_sem.at[block]
                if (d, pc) == (0, 1):
                    pltpu.make_async_copy(src, dst, sem).start()
                else:
                    pltpu.make_async_remote_copy(
                        src_ref=src, dst_ref=dst, send_sem=sd_sem, recv_sem=sem,
                        device_id=device(x, yy, z, pc), device_id_type=MESH,
                    ).start()

    @pl.when(core == 1)
    def _():
        first(0, x, True).start()
        first(0, x, False).start()

    for d, cc in zpeers:
        pc = other(cc)
        remote(qsrc.at[pc], qbuf.at[2 * z + cc], q_sem, device(x, y, wrap(z + d), pc))

    def hop(i, slot, g, to_right):
        sem = xr_sem if to_right else xl_sem
        ref = kvbuf.at[slot, pl.ds(2 * g, 2)]
        return pltpu.make_async_remote_copy(
            src_ref=ref, dst_ref=ref, send_sem=sem.at[0, i], recv_sem=sem.at[1, i],
            device_id=right if to_right else left, device_id_type=MESH,
        )

    row = lax.broadcasted_iota(jnp.int32, (32, 2048), 0)
    col = lax.broadcasted_iota(jnp.int32, (32, 2048), 1)
    base_ok = jnp.logical_and((col & 1) == 0, ((col >> 1) & 1) == ((row >> 3) & 1))
    reach = (col >> 2) - (row >> 4)

    def suffix(n):
        kv = sufbuf[n]
        qn = q_ref[:, n].reshape(32, HD)
        s = lax.dot_general(qn, kv, (((1,), (1,)), ((), ())), preferred_element_type=F32)
        ok = jnp.logical_and(base_ok, reach <= len_ref[n])
        s = jnp.where(ok, s, -jnp.inf)
        mx = jnp.max(s, axis=1, keepdims=True)
        p = jnp.exp2((s - mx) * (SCALE * LOG2E))
        sm = jnp.sum(p, axis=1, keepdims=True)
        pb = pltpu.roll(p, 1, 1).astype(BF16)
        a = jnp.dot(pb, kv, preferred_element_type=F32)
        mxb = jnp.broadcast_to(mx * SCALE, (32, HD))
        smb = jnp.broadcast_to(sm, (32, HD))
        for t in range(2):
            for k in range(2):
                lo = 16 * t + 8 * k
                sacc[k, 4 * t + n] = a[lo : lo + 8]
                smax[k, 4 * t + n] = mxb[lo : lo + 8]
                ssum[k, 4 * t + n] = smb[lo : lo + 8]

    def unit(sa, ga, sb, gb, first=False, after=None):
        def part(slot, g, which):
            return kvbuf[slot, pl.ds(2 * g, 2), which].reshape(96, HD)

        k = jnp.concatenate([part(sa, ga, 0), part(sb, gb, 0)], axis=0)
        v = jnp.concatenate([part(sa, ga, 1), part(sb, gb, 1)], axis=0)
        attend(k, v, first, after)

    def late_unit(sa, sb):
        for slot in (sa, sb):
            pltpu.make_async_copy(kvs.at[slot], kvs.at[slot], s_sem.at[slot]).wait()

        def part(slot, which):
            return kvs[slot, :, which].reshape(128, HD)

        k = jnp.concatenate([part(sa, 0), part(sb, 0)], axis=0)
        v = jnp.concatenate([part(sa, 1), part(sb, 1)], axis=0)
        attend(k, v)

    def attend(k, v, first=False, after=None):
        rows = k.shape[0]
        v = v.T

        def scores(j):
            q = qbuf[4 * j : 4 * j + 4].reshape(256, HD)
            return lax.dot_general(k, q, (((1,), (1,)), ((), ())), preferred_element_type=F32)

        def weigh(j, s):
            r = pl.ds(256 * j, 256)
            new = jnp.max(s, axis=0, keepdims=True)
            keep = None
            if not first:
                old = top[:, r]
                new = jnp.maximum(old, new)
                keep = jnp.exp2((old - new) * (SCALE * LOG2E))
            p = jnp.exp2((s - new) * (SCALE * LOG2E))
            part_sum = jnp.sum(p.reshape(rows // 8, 8, 256), axis=0)
            if not first:
                part_sum = tot[:, r] * keep + part_sum
            top[:, r] = new
            tot[:, r] = part_sum
            return p.astype(BF16), keep

        def gather(j, p, keep):
            r = pl.ds(256 * j, 256)
            o = jnp.dot(v, p, preferred_element_type=F32)
            acc[:, r] = o if first else acc[:, r] * keep + o
            if after:
                after(j)

        js = (0, 1, 2, 3)
        s = scores(js[0])
        late = None
        for i, j in enumerate(js):
            s_next = scores(js[i + 1]) if i < 3 else None
            if late:
                gather(*late)
            late = (j, *weigh(j, s))
            s = s_next
        gather(*late)

    for g in range(4):
        piece = kvbuf.at[x, pl.ds(2 * g, 2)]
        pltpu.make_async_copy(piece, piece, y_sem.at[g]).wait()
        hop(g, x, g, True).start()
        hop(g, x, g, False).start()

        @pl.when(core == 1)
        def _():
            if g == 0:
                spread(x, own=True)
            for to_right in (True, False):
                if g < 3 or to_right:
                    block = wrap(x - g - 1) if to_right else wrap(x + g + 1)
                    first(g, block, to_right).wait_recv()
                    if g < (3 if to_right else 2):
                        first(g + 1, block, to_right).start()
                    spread(block)

        if g == 0:
            fetch[2].wait()
            fetch[3].wait()
        if g < 2:
            suffix(2 * g)
            suffix(2 * g + 1)
    pltpu.make_async_copy(qbuf.at[pl.ds(1, 15)], qbuf.at[pl.ds(1, 15)], q_sem).wait()
    unit(x, 0, x, 1, first=True)
    unit(x, 2, x, 3)

    def middle(i, carry):
        h = lax.div(i, 4) + 1
        g = lax.rem(i, 4)
        sl, sr = wrap(x - h), wrap(x + h)
        hop(i, sl, g, True).wait_recv()

        @pl.when(jnp.logical_or(h < 3, g < 2))
        def _():
            hop(i + 4, sl, g, True).start()

        hop(i, sr, g, False).wait_recv()

        @pl.when(h < 3)
        def _():
            hop(i + 4, sr, g, False).start()

        @pl.when(jnp.logical_and(h == 3, g >= 2))
        def _():
            hop(i + 2, sr, g, False).start()

        unit(sl, g, sr, g)
        return carry

    lax.fori_loop(0, 8, middle, 0)
    late_unit(x, wrap(x - 1))
    lax.fori_loop(8, 12, middle, 0)
    late_unit(wrap(x + 1), wrap(x - 2))
    late_unit(wrap(x + 2), wrap(x - 3))
    def finish(plane):
        r = pl.ds(128 * plane, 128)
        whole = jnp.sum(tot[:, r], axis=0, keepdims=True)
        lsrc[plane] = top[:, r] * SCALE + jnp.log(whole)
        osrc[pl.ds(2 * plane, 2)] = (acc[:, r] / whole).T.astype(BF16).reshape(2, 64, HD)

    def give(plane):
        for cc in range(2):

            def send():
                for src, dst, sem in (
                    (lsrc.at[plane], lbuf.at[2 * z + cc], l_sem),
                    (osrc.at[2 * plane + cc], obuf.at[2 * z + cc], o_sem),
                ):
                    pltpu.make_async_remote_copy(
                        src_ref=src, dst_ref=dst, send_sem=sem.at[0], recv_sem=sem.at[1],
                        device_id=device(x, y, plane, other(cc)), device_id_type=MESH,
                    ).start()

            if cc:
                send()
            else:
                pl.when(z != plane)(send)

    ready = []

    def after(j):
        held = list(ready)
        ready.clear()
        for plane in (2 * j, 2 * j + 1):
            finish(plane)
            ready.append(plane)
        for plane in held:
            give(plane)

    far = wrap(x + 4)
    for g in range(2):
        hop(12 + g, far, g, True).wait_recv()
        hop(12 + g, far, g + 2, False).wait_recv()
        unit(far, g, far, g + 2, after=after if g else None)
        if g == 0:
            late_unit(wrap(x + 3), far)
    obuf[2 * z] = osrc[2 * z]
    lbuf[2 * z] = lsrc[z]
    for plane in ready:
        give(plane)

    def all_of(ref, sem):
        rest = ref.at[pl.ds(0, 15)]
        return pltpu.make_async_copy(rest, rest, sem)

    all_of(lbuf, l_sem.at[1]).wait()
    all_of(obuf, o_sem.at[1]).wait()
    for kk in range(2):
        k = other(kk)
        eye = lax.broadcasted_iota(jnp.int32, (64, HD), 0) + 64 * kk == lax.broadcasted_iota(
            jnp.int32, (64, HD), 1
        )
        sx = smax[k].reshape(64, HD)
        lses = []
        for d in range(RING):
            spread = jnp.where(eye, lbuf[2 * d + kk], 0.0)
            lses.append(jnp.sum(spread, axis=1, keepdims=True))
        best = sx
        for v in lses:
            best = jnp.maximum(best, v)
        w = jnp.exp2((sx - best) * LOG2E)
        num = w * sacc[k].reshape(64, HD)
        den = w * ssum[k].reshape(64, HD)
        for d in range(RING):
            w = jnp.exp2((lses[d] - best) * LOG2E)
            num = num + w * obuf[2 * d + kk].astype(F32)
            den = den + w
        ob[k] = (num / den).reshape(8, 8, HD)
    both = jnp.stack([ob[0], ob[1]], axis=1).reshape(8, 16, HD)
    out_ref[...] = both.astype(BF16).reshape(2, 4, 16, HD)

    for copy in sends:
        copy.wait_send()

    @pl.when(core == 0)
    def _():
        all_of(qbuf, ys_sem).wait()

    @pl.when(core == 1)
    def _():
        all_of(xbuf, ys_sem).wait()
        block = kvbuf.at[pl.ds(0, 5)]
        pltpu.make_async_copy(block, block, sd_sem).wait()
        for i in range(4):
            first(i, x, True).wait_send()
            if i < 3:
                first(i, x, False).wait_send()

    all_of(lbuf, l_sem.at[0]).wait()
    all_of(obuf, o_sem.at[0]).wait()

    def drain(i, carry):
        hop(i, x, 0, True).wait_send()
        hop(i, x, 0, False).wait_send()
        return carry

    lax.fori_loop(0, 14, drain, 0)


def local(prefix_kv, queries, suffix_cache, suffix_lengths):
    vmem = pl.BlockSpec(memory_space=pltpu.VMEM)
    hbm = pl.BlockSpec(memory_space=pltpu.HBM)
    dma = pltpu.SemaphoreType.DMA
    return pl.pallas_call(
        kernel,
        out_shape=pltpu.VMEM(queries.shape, BF16),
        in_specs=[
            hbm, hbm, hbm, hbm,
        ],
        out_specs=vmem,
        scratch_shapes=[
            pltpu.VMEM((256, HD), BF16),
            pltpu.VMEM((2, 4, 16, HD), BF16),
            pltpu.SMEM((4,), jnp.int32),
            pltpu.VMEM((8, 8, 2, 48, HD), BF16),
            pltpu.VMEM((8, 8, 2, 16, HD), BF16),
            pltpu.VMEM((32, 2, 16, HD), BF16),
            pltpu.VMEM((256, HD), F32),
            pltpu.VMEM((4, 2, 32, HD), BF16),
            pltpu.VMEM((2, 64, HD), BF16),
            pltpu.VMEM((16, 64, HD), BF16),
            pltpu.VMEM((4, 2048, HD), BF16),
            pltpu.VMEM((1, 1024), F32),
            pltpu.VMEM((8, 1024), F32),
            pltpu.VMEM((HD, 1024), F32),
            pltpu.VMEM((16, 64, HD), BF16),
            pltpu.VMEM((8, 1, HD), F32),
            pltpu.VMEM((16, 64, HD), BF16),
            pltpu.VMEM((16, 1, HD), F32),
            pltpu.VMEM((2, 8, 8, HD), F32),
            pltpu.VMEM((2, 8, 8, HD), F32),
            pltpu.VMEM((2, 8, 8, HD), F32),
            pltpu.VMEM((2, 8, 8, HD), F32),
            dma((4,)), dma((15,)), dma, dma((2, 2, 4)), dma, dma((8,)), dma((4,)), dma, dma((2, 14)), dma((2, 14)), dma((2,)), dma((2,)),
        ],
        compiler_params=pltpu.CompilerParams(
            collective_id=0, has_side_effects=True, vmem_limit_bytes=66961408
        ),
    )(
        *(
            pltpu.with_memory_space_constraint(a, pltpu.HBM)
            for a in (
                prefix_kv.reshape(256, HD), queries, suffix_lengths,
                suffix_cache.reshape(4, 2048, HD),
            )
        ),
    )


def solution(mesh):
    return jax.shard_map(
        local,
        mesh=mesh,
        in_specs=(
            P(("rep", "ctx", "head", "pool"), None, None, None),
            P(None, ("rep", "ctx", "pool"), "head", None),
            P(("rep", "ctx", "pool"), None, "head", None, None),
            P(("rep", "ctx", "pool")),
        ),
        out_specs=P(None, ("rep", "ctx", "pool"), "head", None),
        check_vma=False,
    )
```

```python
import functools
import math

import jax
import jax.numpy as jnp
from jax import lax
from jax.experimental import pallas as pl
from jax.experimental.pallas import tpu as pltpu
from jax.sharding import PartitionSpec as P

MESH = pl.DeviceIdType.MESH
F32 = jnp.float32
BF16 = jnp.bfloat16
HD = 128
RING = 8
SCALE = 1.0 / math.sqrt(HD)
LOG2E = 1.0 / math.log(2.0)
ORDER = (0, 1, 7, 2, 6, 3, 5, 4)


def wrap(v):
    return lax.rem(v + 2 * RING, RING)


def kernel(
    pre_hbm, q_hbm, len_hbm, suf_hbm, out_ref,
    pre_ref, q_ref, len_ref, kvbuf, kvs, xbuf, kvf, kvsrc, qsrc, qbuf, sufbuf, top, tot, acc, osrc, lsrc, obuf, lbuf,
    sacc, smax, ssum, ob,
    in_sem, send_sem, ys_sem, f_sem, sd_sem, s_sem, y_sem, q_sem, xr_sem, xl_sem, o_sem, l_sem,
):
    x = lax.axis_index("rep")
    c = lax.axis_index("ctx")
    hd = lax.axis_index("head")
    core = lax.axis_index("pool")
    z = lax.div(c, 4)
    y = lax.rem(c, 4) * 2 + hd

    def device(xx, yy, zz, cc):
        return (xx, zz * 4 + lax.div(yy, 2), lax.rem(yy, 2), cc)

    ypeers = [(i, d, cc) for i, d in enumerate(ORDER) for cc in (0, 1) if (d, cc) != (0, 0)]
    zpeers = [(d, cc) for d in ORDER for cc in (0, 1) if (d, cc) != (0, 0)]

    def other(cc):
        return lax.rem(core + cc, 2)

    fetch = [
        pltpu.make_async_copy(src, dst, in_sem.at[i])
        for i, (src, dst) in enumerate(
            [(pre_hbm, pre_ref), (q_hbm, q_ref), (len_hbm, len_ref), (suf_hbm, sufbuf)]
        )
    ]
    for copy in fetch:
        copy.start()

    barrier = pltpu.get_barrier_semaphore()
    greet = [device(x, wrap(y + d), z, other(cc)) for _, d, cc in ypeers]
    greet += [device(x, y, wrap(z + d), other(cc)) for d, cc in zpeers if d]
    greet += [device(wrap(x + 1), y, z, core), device(wrap(x - 1), y, z, core)]
    for dev in greet[14::-1] + greet[:14:-1]:
        pl.semaphore_signal(barrier, inc=1, device_id=dev, device_id_type=MESH)

    fetch[0].wait()
    fetch[1].wait()
    kvf[...] = pre_ref[...].astype(F32)
    for r in range(8):
        kvsrc[r // 2, r % 2] = kvf[pl.ds(r, 32, stride=8), :].astype(BF16)
    my_head = 2 * hd + core
    q8 = q_ref[...].reshape(8, 16, HD).astype(F32)
    for k in range(2):
        qsrc[k] = q8[:, 8 * k : 8 * k + 8, :].reshape(64, HD).astype(BF16)
    qbuf[2 * z] = qsrc[core]

    pl.semaphore_wait(barrier, len(greet))

    sends = []

    def remote(src, dst, recv, dev):
        copy = pltpu.make_async_remote_copy(
            src_ref=src, dst_ref=dst, send_sem=send_sem.at[len(sends)], recv_sem=recv,
            device_id=dev, device_id_type=MESH,
        )
        copy.start()
        sends.append(copy)

    slot_of = {d: i for i, d in enumerate(ORDER)}
    right, left = device(wrap(x + 1), y, z, core), device(wrap(x - 1), y, z, core)

    for cr, (src_rows, dst_rows) in enumerate(((32, 0), (16, 32))):

        @pl.when(core == cr)
        def _():
            for d in ORDER:
                for pc in (cr, 1 - cr):
                    yy = wrap(y + d)
                    src = kvsrc.at[2 * lax.rem(yy, 2) + pc, :, pl.ds(0, src_rows)]
                    slot = slot_of[(-d) % RING]
                    dst = kvbuf.at[x, slot, :, pl.ds(dst_rows, src_rows)]
                    sem = y_sem.at[slot // 2]
                    if (d, pc) == (0, cr):
                        pltpu.make_async_copy(src, dst, sem).start()
                    else:
                        pltpu.make_async_remote_copy(
                            src_ref=src, dst_ref=dst, send_sem=ys_sem, recv_sem=sem,
                            device_id=device(x, yy, z, pc), device_id_type=MESH,
                        ).start()

    late_rows = pl.ds(16, 16)

    def first(i, block, to_right):
        way = 0 if to_right else 1
        ref = xbuf.at[pl.ds(4 * block, 4)]
        return pltpu.make_async_remote_copy(
            src_ref=kvsrc.at[:, :, late_rows] if i == 0 else ref, dst_ref=ref,
            send_sem=f_sem.at[way, 0, i], recv_sem=f_sem.at[way, 1, i],
            device_id=right if to_right else left, device_id_type=MESH,
        )

    def spread(block, own=False):
        for d in ORDER:
            yy = wrap(y + d)
            slot = slot_of[(-d) % RING]
            for pc in (1, 0):
                head = 2 * lax.rem(yy, 2) + pc
                src = kvsrc.at[head, :, late_rows] if own else xbuf.at[4 * block + head]
                dst, sem = kvs.at[block, slot], s_sem.at[block]
                if (d, pc) == (0, 1):
                    pltpu.make_async_copy(src, dst, sem).start()
                else:
                    pltpu.make_async_remote_copy(
                        src_ref=src, dst_ref=dst, send_sem=sd_sem, recv_sem=sem,
                        device_id=device(x, yy, z, pc), device_id_type=MESH,
                    ).start()

    @pl.when(core == 1)
    def _():
        first(0, x, True).start()
        first(0, x, False).start()

    for d, cc in zpeers:
        pc = other(cc)
        remote(qsrc.at[pc], qbuf.at[2 * z + cc], q_sem, device(x, y, wrap(z + d), pc))

    def hop(i, slot, g, to_right):
        sem = xr_sem if to_right else xl_sem
        ref = kvbuf.at[slot, pl.ds(2 * g, 2)]
        return pltpu.make_async_remote_copy(
            src_ref=ref, dst_ref=ref, send_sem=sem.at[0, i], recv_sem=sem.at[1, i],
            device_id=right if to_right else left, device_id_type=MESH,
        )

    row = lax.broadcasted_iota(jnp.int32, (32, 2048), 0)
    col = lax.broadcasted_iota(jnp.int32, (32, 2048), 1)
    base_ok = jnp.logical_and((col & 1) == 0, ((col >> 1) & 1) == ((row >> 3) & 1))
    reach = (col >> 2) - (row >> 4)

    def suffix(n):
        kv = sufbuf[n]
        qn = q_ref[:, n].reshape(32, HD)
        s = lax.dot_general(qn, kv, (((1,), (1,)), ((), ())), preferred_element_type=F32)
        ok = jnp.logical_and(base_ok, reach <= len_ref[n])
        s = jnp.where(ok, s, -jnp.inf)
        mx = jnp.max(s, axis=1, keepdims=True)
        p = jnp.exp2((s - mx) * (SCALE * LOG2E))
        sm = jnp.sum(p, axis=1, keepdims=True)
        pb = pltpu.roll(p, 1, 1).astype(BF16)
        a = jnp.dot(pb, kv, preferred_element_type=F32)
        mxb = jnp.broadcast_to(mx * SCALE, (32, HD))
        smb = jnp.broadcast_to(sm, (32, HD))
        for t in range(2):
            for k in range(2):
                lo = 16 * t + 8 * k
                sacc[k, 4 * t + n] = a[lo : lo + 8]
                smax[k, 4 * t + n] = mxb[lo : lo + 8]
                ssum[k, 4 * t + n] = smb[lo : lo + 8]

    def unit(sa, ga, sb, gb, first=False, after=None):
        def part(slot, g, which):
            return kvbuf[slot, pl.ds(2 * g, 2), which].reshape(96, HD)

        k = jnp.concatenate([part(sa, ga, 0), part(sb, gb, 0)], axis=0)
        v = jnp.concatenate([part(sa, ga, 1), part(sb, gb, 1)], axis=0)
        attend(k, v, first, after)

    def late_unit(sa, sb):
        for slot in (sa, sb):
            pltpu.make_async_copy(kvs.at[slot], kvs.at[slot], s_sem.at[slot]).wait()

        def part(slot, which):
            return kvs[slot, :, which].reshape(128, HD)

        k = jnp.concatenate([part(sa, 0), part(sb, 0)], axis=0)
        v = jnp.concatenate([part(sa, 1), part(sb, 1)], axis=0)
        attend(k, v)

    def attend(k, v, first=False, after=None):
        rows = k.shape[0]
        v = v.T

        def scores(j):
            q = qbuf[4 * j : 4 * j + 4].reshape(256, HD)
            return lax.dot_general(k, q, (((1,), (1,)), ((), ())), preferred_element_type=F32)

        def weigh(j, s):
            r = pl.ds(256 * j, 256)
            new = jnp.max(s, axis=0, keepdims=True)
            keep = None
            if not first:
                old = top[:, r]
                new = jnp.maximum(old, new)
                keep = jnp.exp2((old - new) * (SCALE * LOG2E))
            p = jnp.exp2((s - new) * (SCALE * LOG2E))
            part_sum = jnp.sum(p.reshape(rows // 8, 8, 256), axis=0)
            if not first:
                part_sum = tot[:, r] * keep + part_sum
            top[:, r] = new
            tot[:, r] = part_sum
            return p.astype(BF16), keep

        def gather(j, p, keep):
            r = pl.ds(256 * j, 256)
            o = jnp.dot(v, p, preferred_element_type=F32)
            acc[:, r] = o if first else acc[:, r] * keep + o
            if after:
                after(j)

        js = (0, 1, 2, 3)
        s = scores(js[0])
        late = None
        for i, j in enumerate(js):
            s_next = scores(js[i + 1]) if i < 3 else None
            if late:
                gather(*late)
            late = (j, *weigh(j, s))
            s = s_next
        gather(*late)

    for g in range(4):
        piece = kvbuf.at[x, pl.ds(2 * g, 2)]
        pltpu.make_async_copy(piece, piece, y_sem.at[g]).wait()
        hop(g, x, g, True).start()
        hop(g, x, g, False).start()

        @pl.when(core == 1)
        def _():
            if g == 0:
                spread(x, own=True)
            for to_right in (True, False):
                if g < 3 or to_right:
                    block = wrap(x - g - 1) if to_right else wrap(x + g + 1)
                    first(g, block, to_right).wait_recv()
                    if g < (3 if to_right else 2):
                        first(g + 1, block, to_right).start()
                    spread(block)

        if g == 0:
            fetch[2].wait()
            fetch[3].wait()
        if g < 2:
            suffix(2 * g)
            suffix(2 * g + 1)
    pltpu.make_async_copy(qbuf.at[pl.ds(1, 15)], qbuf.at[pl.ds(1, 15)], q_sem).wait()
    unit(x, 0, x, 1, first=True)
    unit(x, 2, x, 3)

    def middle(i, carry):
        h = lax.div(i, 4) + 1
        g = lax.rem(i, 4)
        sl, sr = wrap(x - h), wrap(x + h)
        hop(i, sl, g, True).wait_recv()

        @pl.when(jnp.logical_or(h < 3, g < 2))
        def _():
            hop(i + 4, sl, g, True).start()

        hop(i, sr, g, False).wait_recv()

        @pl.when(h < 3)
        def _():
            hop(i + 4, sr, g, False).start()

        @pl.when(jnp.logical_and(h == 3, g >= 2))
        def _():
            hop(i + 2, sr, g, False).start()

        unit(sl, g, sr, g)
        return carry

    lax.fori_loop(0, 8, middle, 0)
    late_unit(x, wrap(x - 1))
    lax.fori_loop(8, 12, middle, 0)
    late_unit(wrap(x + 1), wrap(x - 2))
    late_unit(wrap(x + 2), wrap(x - 3))
    def finish(plane):
        r = pl.ds(128 * plane, 128)
        whole = jnp.sum(tot[:, r], axis=0, keepdims=True)
        lsrc[plane] = top[:, r] * SCALE + jnp.log(whole)
        osrc[pl.ds(2 * plane, 2)] = (acc[:, r] / whole).T.astype(BF16).reshape(2, 64, HD)

    def give(plane):
        for cc in range(2):

            def send():
                for src, dst, sem in (
                    (lsrc.at[plane], lbuf.at[2 * z + cc], l_sem),
                    (osrc.at[2 * plane + cc], obuf.at[2 * z + cc], o_sem),
                ):
                    pltpu.make_async_remote_copy(
                        src_ref=src, dst_ref=dst, send_sem=sem.at[0], recv_sem=sem.at[1],
                        device_id=device(x, y, plane, other(cc)), device_id_type=MESH,
                    ).start()

            if cc:
                send()
            else:
                pl.when(z != plane)(send)

    ready = []

    def after(j):
        for plane in (2 * j, 2 * j + 1):
            finish(plane)
            if ready:
                give(ready.pop())
            ready.append(plane)

    far = wrap(x + 4)
    for g in range(2):
        hop(12 + g, far, g, True).wait_recv()
        hop(12 + g, far, g + 2, False).wait_recv()
        unit(far, g, far, g + 2, after=after if g else None)
        if g == 0:
            late_unit(wrap(x + 3), far)
    obuf[2 * z] = osrc[2 * z]
    lbuf[2 * z] = lsrc[z]
    for plane in ready:
        give(plane)

    def all_of(ref, sem):
        rest = ref.at[pl.ds(0, 15)]
        return pltpu.make_async_copy(rest, rest, sem)

    all_of(lbuf, l_sem.at[1]).wait()
    shares = []
    for kk in range(2):
        k = other(kk)
        eye = lax.broadcasted_iota(jnp.int32, (64, HD), 0) + 64 * kk == lax.broadcasted_iota(
            jnp.int32, (64, HD), 1
        )
        sx = smax[k].reshape(64, HD)
        lses = [
            jnp.sum(jnp.where(eye, lbuf[2 * d + kk], 0.0), axis=1, keepdims=True)
            for d in range(RING)
        ]
        best = sx
        for v in lses:
            best = jnp.maximum(best, v)
        own = jnp.exp2((sx - best) * LOG2E)
        ws = [jnp.exp2((v - best) * LOG2E) for v in lses]
        den = own * ssum[k].reshape(64, HD)
        for w in ws:
            den = den + w
        shares.append((own * sacc[k].reshape(64, HD), ws, den))
    all_of(obuf, o_sem.at[1]).wait()
    for kk, (num, ws, den) in enumerate(shares):
        for d, w in enumerate(ws):
            num = num + w * obuf[2 * d + kk].astype(F32)
        ob[other(kk)] = (num / den).reshape(8, 8, HD)
    both = jnp.stack([ob[0], ob[1]], axis=1).reshape(8, 16, HD)
    out_ref[...] = both.astype(BF16).reshape(2, 4, 16, HD)

    for copy in sends:
        copy.wait_send()

    @pl.when(core == 0)
    def _():
        all_of(qbuf, ys_sem).wait()

    @pl.when(core == 1)
    def _():
        all_of(xbuf, ys_sem).wait()
        block = kvbuf.at[pl.ds(0, 5)]
        pltpu.make_async_copy(block, block, sd_sem).wait()
        for i in range(4):
            first(i, x, True).wait_send()
            if i < 3:
                first(i, x, False).wait_send()

    all_of(lbuf, l_sem.at[0]).wait()
    all_of(obuf, o_sem.at[0]).wait()

    def drain(i, carry):
        hop(i, x, 0, True).wait_send()
        hop(i, x, 0, False).wait_send()
        return carry

    lax.fori_loop(0, 14, drain, 0)


def local(prefix_kv, queries, suffix_cache, suffix_lengths):
    vmem = pl.BlockSpec(memory_space=pltpu.VMEM)
    hbm = pl.BlockSpec(memory_space=pltpu.HBM)
    dma = pltpu.SemaphoreType.DMA
    return pl.pallas_call(
        kernel,
        out_shape=pltpu.VMEM(queries.shape, BF16),
        in_specs=[
            hbm, hbm, hbm, hbm,
        ],
        out_specs=vmem,
        scratch_shapes=[
            pltpu.VMEM((256, HD), BF16),
            pltpu.VMEM((2, 4, 16, HD), BF16),
            pltpu.SMEM((4,), jnp.int32),
            pltpu.VMEM((8, 8, 2, 48, HD), BF16),
            pltpu.VMEM((8, 8, 2, 16, HD), BF16),
            pltpu.VMEM((32, 2, 16, HD), BF16),
            pltpu.VMEM((256, HD), F32),
            pltpu.VMEM((4, 2, 32, HD), BF16),
            pltpu.VMEM((2, 64, HD), BF16),
            pltpu.VMEM((16, 64, HD), BF16),
            pltpu.VMEM((4, 2048, HD), BF16),
            pltpu.VMEM((1, 1024), F32),
            pltpu.VMEM((8, 1024), F32),
            pltpu.VMEM((HD, 1024), F32),
            pltpu.VMEM((16, 64, HD), BF16),
            pltpu.VMEM((8, 1, HD), F32),
            pltpu.VMEM((16, 64, HD), BF16),
            pltpu.VMEM((16, 1, HD), F32),
            pltpu.VMEM((2, 8, 8, HD), F32),
            pltpu.VMEM((2, 8, 8, HD), F32),
            pltpu.VMEM((2, 8, 8, HD), F32),
            pltpu.VMEM((2, 8, 8, HD), F32),
            dma((4,)), dma((15,)), dma, dma((2, 2, 4)), dma, dma((8,)), dma((4,)), dma, dma((2, 14)), dma((2, 14)), dma((2,)), dma((2,)),
        ],
        compiler_params=pltpu.CompilerParams(
            collective_id=0, has_side_effects=True, vmem_limit_bytes=66961408
        ),
    )(
        *(
            pltpu.with_memory_space_constraint(a, pltpu.HBM)
            for a in (
                prefix_kv.reshape(256, HD), queries, suffix_lengths,
                suffix_cache.reshape(4, 2048, HD),
            )
        ),
    )


def solution(mesh):
    return jax.shard_map(
        local,
        mesh=mesh,
        in_specs=(
            P(("rep", "ctx", "head", "pool"), None, None, None),
            P(None, ("rep", "ctx", "pool"), "head", None),
            P(("rep", "ctx", "pool"), None, "head", None, None),
            P(("rep", "ctx", "pool")),
        ),
        out_specs=P(None, ("rep", "ctx", "pool"), "head", None),
        check_vma=False,
    )
```

```python
import functools
import math

import jax
import jax.numpy as jnp
from jax import lax
from jax.experimental import pallas as pl
from jax.experimental.pallas import tpu as pltpu
from jax.sharding import PartitionSpec as P

MESH = pl.DeviceIdType.MESH
F32 = jnp.float32
BF16 = jnp.bfloat16
HD = 128
RING = 8
SCALE = 1.0 / math.sqrt(HD)
LOG2E = 1.0 / math.log(2.0)
ORDER = (0, 1, 7, 2, 6, 3, 5, 4)


def wrap(v):
    return lax.rem(v + 2 * RING, RING)


def kernel(
    pre_hbm, q_hbm, len_hbm, suf_hbm, out_ref,
    pre_ref, q_ref, len_ref, kvbuf, kvs, xbuf, kvf, kvsrc, qsrc, qbuf, sufbuf, top, tot, acc, osrc, lsrc, obuf, lbuf,
    sacc, smax, ssum, ob,
    in_sem, send_sem, ys_sem, f_sem, sd_sem, s_sem, y_sem, q_sem, xr_sem, xl_sem, o_sem, l_sem,
):
    x = lax.axis_index("rep")
    c = lax.axis_index("ctx")
    hd = lax.axis_index("head")
    core = lax.axis_index("pool")
    z = lax.div(c, 4)
    y = lax.rem(c, 4) * 2 + hd

    def device(xx, yy, zz, cc):
        return (xx, zz * 4 + lax.div(yy, 2), lax.rem(yy, 2), cc)

    ypeers = [(i, d, cc) for i, d in enumerate(ORDER) for cc in (0, 1) if (d, cc) != (0, 0)]
    zpeers = [(d, cc) for d in ORDER for cc in (0, 1) if (d, cc) != (0, 0)]

    def other(cc):
        return lax.rem(core + cc, 2)

    fetch = [
        pltpu.make_async_copy(src, dst, in_sem.at[i])
        for i, (src, dst) in enumerate(
            [(pre_hbm, pre_ref), (q_hbm, q_ref), (len_hbm, len_ref), (suf_hbm, sufbuf)]
        )
    ]
    for copy in fetch:
        copy.start()

    barrier = pltpu.get_barrier_semaphore()
    greet = [device(x, wrap(y + d), z, other(cc)) for _, d, cc in ypeers]
    greet += [device(x, y, wrap(z + d), other(cc)) for d, cc in zpeers if d]
    greet += [device(wrap(x + 1), y, z, core), device(wrap(x - 1), y, z, core)]
    for dev in greet[14::-1] + greet[:14:-1]:
        pl.semaphore_signal(barrier, inc=1, device_id=dev, device_id_type=MESH)

    fetch[0].wait()
    fetch[1].wait()
    kvf[...] = pre_ref[...].astype(F32)
    for r in range(8):
        kvsrc[r // 2, r % 2] = kvf[pl.ds(r, 32, stride=8), :].astype(BF16)
    my_head = 2 * hd + core
    q8 = q_ref[...].reshape(8, 16, HD).astype(F32)
    for k in range(2):
        qsrc[k] = q8[:, 8 * k : 8 * k + 8, :].reshape(64, HD).astype(BF16)
    qbuf[2 * z] = qsrc[core]

    pl.semaphore_wait(barrier, len(greet))

    sends = []

    def remote(src, dst, recv, dev):
        copy = pltpu.make_async_remote_copy(
            src_ref=src, dst_ref=dst, send_sem=send_sem.at[len(sends)], recv_sem=recv,
            device_id=dev, device_id_type=MESH,
        )
        copy.start()
        sends.append(copy)

    slot_of = {d: i for i, d in enumerate(ORDER)}
    right, left = device(wrap(x + 1), y, z, core), device(wrap(x - 1), y, z, core)

    for cr, (src_rows, dst_rows) in enumerate(((32, 0), (16, 32))):

        @pl.when(core == cr)
        def _():
            for d in ORDER:
                for pc in (cr, 1 - cr):
                    yy = wrap(y + d)
                    src = kvsrc.at[2 * lax.rem(yy, 2) + pc, :, pl.ds(0, src_rows)]
                    slot = slot_of[(-d) % RING]
                    dst = kvbuf.at[x, slot, :, pl.ds(dst_rows, src_rows)]
                    sem = y_sem.at[slot // 2]
                    if (d, pc) == (0, cr):
                        pltpu.make_async_copy(src, dst, sem).start()
                    else:
                        pltpu.make_async_remote_copy(
                            src_ref=src, dst_ref=dst, send_sem=ys_sem, recv_sem=sem,
                            device_id=device(x, yy, z, pc), device_id_type=MESH,
                        ).start()

    late_rows = pl.ds(16, 16)

    def first(i, block, to_right):
        way = 0 if to_right else 1
        ref = xbuf.at[pl.ds(4 * block, 4)]
        return pltpu.make_async_remote_copy(
            src_ref=kvsrc.at[:, :, late_rows] if i == 0 else ref, dst_ref=ref,
            send_sem=f_sem.at[way, 0, i], recv_sem=f_sem.at[way, 1, i],
            device_id=right if to_right else left, device_id_type=MESH,
        )

    def spread(block, own=False):
        for d in ORDER:
            yy = wrap(y + d)
            slot = slot_of[(-d) % RING]
            for pc in (1, 0):
                head = 2 * lax.rem(yy, 2) + pc
                src = kvsrc.at[head, :, late_rows] if own else xbuf.at[4 * block + head]
                dst, sem = kvs.at[block, slot], s_sem.at[block]
                if (d, pc) == (0, 1):
                    pltpu.make_async_copy(src, dst, sem).start()
                else:
                    pltpu.make_async_remote_copy(
                        src_ref=src, dst_ref=dst, send_sem=sd_sem, recv_sem=sem,
                        device_id=device(x, yy, z, pc), device_id_type=MESH,
                    ).start()

    @pl.when(core == 1)
    def _():
        first(0, x, True).start()
        first(0, x, False).start()

    for d, cc in zpeers:
        pc = other(cc)
        remote(qsrc.at[pc], qbuf.at[2 * z + cc], q_sem, device(x, y, wrap(z + d), pc))

    def hop(i, slot, g, to_right):
        sem = xr_sem if to_right else xl_sem
        ref = kvbuf.at[slot, pl.ds(2 * g, 2)]
        return pltpu.make_async_remote_copy(
            src_ref=ref, dst_ref=ref, send_sem=sem.at[0, i], recv_sem=sem.at[1, i],
            device_id=right if to_right else left, device_id_type=MESH,
        )

    row = lax.broadcasted_iota(jnp.int32, (32, 2048), 0)
    col = lax.broadcasted_iota(jnp.int32, (32, 2048), 1)
    base_ok = jnp.logical_and((col & 1) == 0, ((col >> 1) & 1) == ((row >> 3) & 1))
    reach = (col >> 2) - (row >> 4)

    def suffix(n):
        kv = sufbuf[n]
        qn = q_ref[:, n].reshape(32, HD)
        s = lax.dot_general(qn, kv, (((1,), (1,)), ((), ())), preferred_element_type=F32)
        ok = jnp.logical_and(base_ok, reach <= len_ref[n])
        s = jnp.where(ok, s, -jnp.inf)
        mx = jnp.max(s, axis=1, keepdims=True)
        p = jnp.exp2((s - mx) * (SCALE * LOG2E))
        sm = jnp.sum(p, axis=1, keepdims=True)
        pb = pltpu.roll(p, 1, 1).astype(BF16)
        a = jnp.dot(pb, kv, preferred_element_type=F32)
        mxb = jnp.broadcast_to(mx * SCALE, (32, HD))
        smb = jnp.broadcast_to(sm, (32, HD))
        for t in range(2):
            for k in range(2):
                lo = 16 * t + 8 * k
                sacc[k, 4 * t + n] = a[lo : lo + 8]
                smax[k, 4 * t + n] = mxb[lo : lo + 8]
                ssum[k, 4 * t + n] = smb[lo : lo + 8]

    def unit(sa, ga, sb, gb, first=False, after=None):
        def part(slot, g, which):
            return kvbuf[slot, pl.ds(2 * g, 2), which].reshape(96, HD)

        k = jnp.concatenate([part(sa, ga, 0), part(sb, gb, 0)], axis=0)
        v = jnp.concatenate([part(sa, ga, 1), part(sb, gb, 1)], axis=0)
        attend(k, v, first, after)

    def late_unit(sa, sb):
        for slot in (sa, sb):
            pltpu.make_async_copy(kvs.at[slot], kvs.at[slot], s_sem.at[slot]).wait()

        def part(slot, which):
            return kvs[slot, :, which].reshape(128, HD)

        k = jnp.concatenate([part(sa, 0), part(sb, 0)], axis=0)
        v = jnp.concatenate([part(sa, 1), part(sb, 1)], axis=0)
        attend(k, v)

    def attend(k, v, first=False, after=None):
        rows = k.shape[0]
        v = v.T

        def scores(j):
            q = qbuf[4 * j : 4 * j + 4].reshape(256, HD)
            return lax.dot_general(k, q, (((1,), (1,)), ((), ())), preferred_element_type=F32)

        def weigh(j, s):
            r = pl.ds(256 * j, 256)
            new = jnp.max(s, axis=0, keepdims=True)
            keep = None
            if not first:
                old = top[:, r]
                new = jnp.maximum(old, new)
                keep = jnp.exp2((old - new) * (SCALE * LOG2E))
            p = jnp.exp2((s - new) * (SCALE * LOG2E))
            part_sum = jnp.sum(p.reshape(rows // 8, 8, 256), axis=0)
            if not first:
                part_sum = tot[:, r] * keep + part_sum
            top[:, r] = new
            tot[:, r] = part_sum
            return p.astype(BF16), keep

        def gather(j, p, keep):
            r = pl.ds(256 * j, 256)
            o = jnp.dot(v, p, preferred_element_type=F32)
            acc[:, r] = o if first else acc[:, r] * keep + o
            if after:
                after(j)

        js = (0, 1, 2, 3)
        s = scores(js[0])
        late = None
        for i, j in enumerate(js):
            s_next = scores(js[i + 1]) if i < 3 else None
            if late:
                gather(*late)
            late = (j, *weigh(j, s))
            s = s_next
        gather(*late)

    for g in range(4):
        piece = kvbuf.at[x, pl.ds(2 * g, 2)]
        pltpu.make_async_copy(piece, piece, y_sem.at[g]).wait()
        hop(g, x, g, True).start()
        hop(g, x, g, False).start()

        @pl.when(core == 1)
        def _():
            if g == 0:
                spread(x, own=True)
            for to_right in (True, False):
                if g < 3 or to_right:
                    block = wrap(x - g - 1) if to_right else wrap(x + g + 1)
                    first(g, block, to_right).wait_recv()
                    if g < (3 if to_right else 2):
                        first(g + 1, block, to_right).start()
                    spread(block)

        if g == 0:
            fetch[2].wait()
            fetch[3].wait()
    pltpu.make_async_copy(qbuf.at[pl.ds(1, 15)], qbuf.at[pl.ds(1, 15)], q_sem).wait()
    unit(x, 0, x, 1, first=True)
    unit(x, 2, x, 3)

    def middle(i, carry):
        h = lax.div(i, 4) + 1
        g = lax.rem(i, 4)
        sl, sr = wrap(x - h), wrap(x + h)
        hop(i, sl, g, True).wait_recv()

        @pl.when(jnp.logical_or(h < 3, g < 2))
        def _():
            hop(i + 4, sl, g, True).start()

        hop(i, sr, g, False).wait_recv()

        @pl.when(h < 3)
        def _():
            hop(i + 4, sr, g, False).start()

        @pl.when(jnp.logical_and(h == 3, g >= 2))
        def _():
            hop(i + 2, sr, g, False).start()

        unit(sl, g, sr, g)
        return carry

    for n in range(4):
        lax.fori_loop(2 * n, 2 * n + 2, middle, 0)
        suffix(n)
    late_unit(x, wrap(x - 1))
    lax.fori_loop(8, 12, middle, 0)
    late_unit(wrap(x + 1), wrap(x - 2))
    late_unit(wrap(x + 2), wrap(x - 3))
    def finish(plane):
        r = pl.ds(128 * plane, 128)
        whole = jnp.sum(tot[:, r], axis=0, keepdims=True)
        lsrc[plane] = top[:, r] * SCALE + jnp.log(whole)
        osrc[pl.ds(2 * plane, 2)] = (acc[:, r] / whole).T.astype(BF16).reshape(2, 64, HD)

    def give(plane):
        for cc in range(2):

            def send():
                for src, dst, sem in (
                    (lsrc.at[plane], lbuf.at[2 * z + cc], l_sem),
                    (osrc.at[2 * plane + cc], obuf.at[2 * z + cc], o_sem),
                ):
                    pltpu.make_async_remote_copy(
                        src_ref=src, dst_ref=dst, send_sem=sem.at[0], recv_sem=sem.at[1],
                        device_id=device(x, y, plane, other(cc)), device_id_type=MESH,
                    ).start()

            if cc:
                send()
            else:
                pl.when(z != plane)(send)

    ready = []

    def after(j):
        for plane in (2 * j, 2 * j + 1):
            finish(plane)
            if ready:
                give(ready.pop())
            ready.append(plane)

    far = wrap(x + 4)
    for g in range(2):
        hop(12 + g, far, g, True).wait_recv()
        hop(12 + g, far, g + 2, False).wait_recv()
        unit(far, g, far, g + 2, after=after if g else None)
        if g == 0:
            late_unit(wrap(x + 3), far)
    obuf[2 * z] = osrc[2 * z]
    lbuf[2 * z] = lsrc[z]
    for plane in ready:
        give(plane)

    def all_of(ref, sem):
        rest = ref.at[pl.ds(0, 15)]
        return pltpu.make_async_copy(rest, rest, sem)

    all_of(lbuf, l_sem.at[1]).wait()
    shares = []
    for kk in range(2):
        k = other(kk)
        eye = lax.broadcasted_iota(jnp.int32, (64, HD), 0) + 64 * kk == lax.broadcasted_iota(
            jnp.int32, (64, HD), 1
        )
        sx = smax[k].reshape(64, HD)
        lses = [
            jnp.sum(jnp.where(eye, lbuf[2 * d + kk], 0.0), axis=1, keepdims=True)
            for d in range(RING)
        ]
        best = sx
        for v in lses:
            best = jnp.maximum(best, v)
        own = jnp.exp2((sx - best) * LOG2E)
        ws = [jnp.exp2((v - best) * LOG2E) for v in lses]
        den = own * ssum[k].reshape(64, HD)
        for w in ws:
            den = den + w
        shares.append((own * sacc[k].reshape(64, HD), ws, den))
    all_of(obuf, o_sem.at[1]).wait()
    for kk, (num, ws, den) in enumerate(shares):
        for d, w in enumerate(ws):
            num = num + w * obuf[2 * d + kk].astype(F32)
        ob[other(kk)] = (num / den).reshape(8, 8, HD)
    both = jnp.stack([ob[0], ob[1]], axis=1).reshape(8, 16, HD)
    out_ref[...] = both.astype(BF16).reshape(2, 4, 16, HD)

    for copy in sends:
        copy.wait_send()

    @pl.when(core == 0)
    def _():
        all_of(qbuf, ys_sem).wait()

    @pl.when(core == 1)
    def _():
        all_of(xbuf, ys_sem).wait()
        block = kvbuf.at[pl.ds(0, 5)]
        pltpu.make_async_copy(block, block, sd_sem).wait()
        for i in range(4):
            first(i, x, True).wait_send()
            if i < 3:
                first(i, x, False).wait_send()

    all_of(lbuf, l_sem.at[0]).wait()
    all_of(obuf, o_sem.at[0]).wait()

    def drain(i, carry):
        hop(i, x, 0, True).wait_send()
        hop(i, x, 0, False).wait_send()
        return carry

    lax.fori_loop(0, 14, drain, 0)


def local(prefix_kv, queries, suffix_cache, suffix_lengths):
    vmem = pl.BlockSpec(memory_space=pltpu.VMEM)
    hbm = pl.BlockSpec(memory_space=pltpu.HBM)
    dma = pltpu.SemaphoreType.DMA
    return pl.pallas_call(
        kernel,
        out_shape=pltpu.VMEM(queries.shape, BF16),
        in_specs=[
            hbm, hbm, hbm, hbm,
        ],
        out_specs=vmem,
        scratch_shapes=[
            pltpu.VMEM((256, HD), BF16),
            pltpu.VMEM((2, 4, 16, HD), BF16),
            pltpu.SMEM((4,), jnp.int32),
            pltpu.VMEM((8, 8, 2, 48, HD), BF16),
            pltpu.VMEM((8, 8, 2, 16, HD), BF16),
            pltpu.VMEM((32, 2, 16, HD), BF16),
            pltpu.VMEM((256, HD), F32),
            pltpu.VMEM((4, 2, 32, HD), BF16),
            pltpu.VMEM((2, 64, HD), BF16),
            pltpu.VMEM((16, 64, HD), BF16),
            pltpu.VMEM((4, 2048, HD), BF16),
            pltpu.VMEM((1, 1024), F32),
            pltpu.VMEM((8, 1024), F32),
            pltpu.VMEM((HD, 1024), F32),
            pltpu.VMEM((16, 64, HD), BF16),
            pltpu.VMEM((8, 1, HD), F32),
            pltpu.VMEM((16, 64, HD), BF16),
            pltpu.VMEM((16, 1, HD), F32),
            pltpu.VMEM((2, 8, 8, HD), F32),
            pltpu.VMEM((2, 8, 8, HD), F32),
            pltpu.VMEM((2, 8, 8, HD), F32),
            pltpu.VMEM((2, 8, 8, HD), F32),
            dma((4,)), dma((15,)), dma, dma((2, 2, 4)), dma, dma((8,)), dma((4,)), dma, dma((2, 14)), dma((2, 14)), dma((2,)), dma((2,)),
        ],
        compiler_params=pltpu.CompilerParams(
            collective_id=0, has_side_effects=True, vmem_limit_bytes=66961408
        ),
    )(
        *(
            pltpu.with_memory_space_constraint(a, pltpu.HBM)
            for a in (
                prefix_kv.reshape(256, HD), queries, suffix_lengths,
                suffix_cache.reshape(4, 2048, HD),
            )
        ),
    )


def solution(mesh):
    return jax.shard_map(
        local,
        mesh=mesh,
        in_specs=(
            P(("rep", "ctx", "head", "pool"), None, None, None),
            P(None, ("rep", "ctx", "pool"), "head", None),
            P(("rep", "ctx", "pool"), None, "head", None, None),
            P(("rep", "ctx", "pool")),
        ),
        out_specs=P(None, ("rep", "ctx", "pool"), "head", None),
        check_vma=False,
    )
```
